512 devices in a mesh: row: 16 (over y, core), col: 32 (over z, x).
Axes of the slice: x: 4, y: 8, z: 8, core: 2. Of those that a mesh axis runs over, the one named last changes fastest.
Arguments:
- grad_out: bfloat16 [2048, 8192], P('col', 'row'), may hold values from -0.09375 to 0.09375
- activations: bfloat16 [2048, 28672], P('row', 'col'), may hold values from -6 to 6
- left_steps: float32 [10, 8192], P(None, 'row')
- left_curves: float32 [10, 8192], P(None, 'row'), as said below
- right_steps: float32 [10, 28672], P(None, 'col')
- right_curves: float32 [10, 28672], P(None, 'col'), as said below
Outputs:
- direction: float32 [8192, 28672], P('row', 'col')
The draws below stay inside these ranges and needn't reach their ends.
Inputs may be any that keep to these rules, and one draw needn't show every extreme that they name: `left_curves`: each curve row is its step row scaled entrywise by positive factors, so every step has a positive inner product with its curve; the last pair is the newest. `right_curves`: as for the output side.
All inputs are finite; a program needn't handle non-finite values.
Results may differ from the reference program's by a relative error of at most 0.0003.
Values may be sent and summed in bfloat16 or wider, within the bound.
No kernel may reach another device: no remote copies, remote signals or barrier semaphores. Data moves between devices by JAX's collectives and lax.ppermute only.
A program may use at most 64 MiB of HBM per device.

```python
import math
import jax
import jax.numpy as jnp
from jax import lax

D = 8192
FF = 28672
TOKENS = 2048
PAIRS = 10


def history(key, width, salt):
    base = jax.random.fold_in(key, salt)
    first, second, third, fourth = jax.random.split(base, 4)
    step_rows = jax.random.normal(first, (PAIRS, width), jnp.float32)
    curvature = jnp.exp(jax.random.uniform(second, (PAIRS, 1), jnp.float32, math.log(0.03), 0.0))
    newest = jax.random.uniform(fourth, (PAIRS, 1), jnp.float32, 0.5, 1.0)
    position = jnp.arange(PAIRS).reshape(PAIRS, 1)
    curvature = jnp.where(position == PAIRS - 1, newest, curvature)
    wobble = jax.random.uniform(third, (PAIRS, width), jnp.float32, -1.0, 1.0)
    return (step_rows, curvature * step_rows * (1.0 + 0.5 * wobble))


def draw_left_steps(key, part):
    return history(key, D, 7)[0]


def draw_left_curves(key, part):
    return history(key, D, 7)[1]


def draw_right_steps(key, part):
    return history(key, FF, 11)[0]


def draw_right_curves(key, part):
    return history(key, FF, 11)[1]


def shard_levels(key, dims, pieces, least, largest):
    gain = 1.0
    for dim, blocks in pieces:
        draws = jax.random.uniform(jax.random.fold_in(jax.random.fold_in(key, 6), dim), (blocks,), jnp.float32, least / len(pieces), largest / len(pieces))
        gain = gain * jnp.repeat(jnp.exp(draws), dims[dim] // blocks).reshape((-1,) + (1,) * (len(dims) - 1 - dim))
    return gain


def noise(rng, shape, scale, most, cuts=(), kind=jnp.bfloat16):
    drawn = scale * jax.random.normal(rng, shape, jnp.float32)
    if cuts:
        drawn = drawn * shard_levels(rng, shape, cuts, -0.22, 0.18)
    return jnp.clip(drawn, -most, most).astype(kind)


def setup_inputs(seed: int = 0) -> dict:
    seeds = jax.random.split(jax.random.key(seed), 7)
    grad_out = noise(seeds[0], (TOKENS, D), 0.015625, 0.09375, ((0, 32), (1, 16)))
    activations = noise(seeds[1], (TOKENS, FF), 1.0, 6.0, ((0, 16), (1, 32)))
    left_steps = draw_left_steps(jax.random.fold_in(seeds[6], 71), 0)
    left_curves = draw_left_curves(jax.random.fold_in(seeds[6], 71), 0)
    right_steps = draw_right_steps(jax.random.fold_in(seeds[6], 71), 0)
    right_curves = draw_right_curves(jax.random.fold_in(seeds[6], 71), 0)
    return dict(grad_out=grad_out, activations=activations, left_steps=left_steps, left_curves=left_curves, right_steps=right_steps, right_curves=right_curves)


HIGH = lax.Precision.HIGHEST


def side_terms(step_rows, curv_rows):
    pair_sy = jnp.dot(step_rows, curv_rows.T, precision=HIGH, preferred_element_type=jnp.float32)
    pair_yy = jnp.dot(curv_rows, curv_rows.T, precision=HIGH, preferred_element_type=jnp.float32)
    return pair_sy, pair_yy


def upper_inverse(upper_tri):
    count = upper_tri.shape[0]
    identity = jnp.eye(count, dtype=upper_tri.dtype)
    inv_rows = [None] * count
    for index in reversed(range(count)):
        running = identity[index]
        for later in range(index + 1, count):
            running = running - upper_tri[index, later] * inv_rows[later]
        inv_rows[index] = running / upper_tri[index, index]
    return jnp.stack(inv_rows, 0)


def compact(pair_sy, pair_yy):
    scaling = pair_sy[-1, -1] / pair_yy[-1, -1]
    upper_tri = jnp.triu(pair_sy)
    inverse = upper_inverse(upper_tri)
    middle = jnp.diag(jnp.diag(pair_sy)) + scaling * pair_yy
    return scaling, inverse, middle


def reference(grad_out, activations, left_steps, left_curves, right_steps, right_curves):
    grad = lax.dot_general(grad_out, activations, (((0,), (0,)), ((), ())), preferred_element_type=jnp.float32)
    l_scale, l_inv, l_mid = compact(*side_terms(left_steps, left_curves))
    r_scale, r_inv, r_mid = compact(*side_terms(right_steps, right_curves))
    proj_steps = jnp.dot(left_steps, grad, precision=HIGH)
    proj_curves = jnp.dot(left_curves, grad, precision=HIGH)
    weighted = jnp.dot(l_inv, proj_steps, precision=HIGH)
    coeffs = jnp.dot(l_inv.T, jnp.dot(l_mid, weighted, precision=HIGH) - l_scale * proj_curves, precision=HIGH)
    lefted = l_scale * grad + jnp.dot(left_steps.T, coeffs, precision=HIGH) - l_scale * jnp.dot(left_curves.T, weighted, precision=HIGH)
    side_steps = jnp.dot(lefted, right_steps.T, precision=HIGH)
    side_curves = jnp.dot(lefted, right_curves.T, precision=HIGH)
    rweighted = jnp.dot(side_steps, r_inv.T, precision=HIGH)
    rcoeffs = jnp.dot(jnp.dot(rweighted, r_mid, precision=HIGH) - r_scale * side_curves, r_inv, precision=HIGH)
    return r_scale * lefted + jnp.dot(rcoeffs, right_steps, precision=HIGH) - r_scale * jnp.dot(rweighted, right_curves, precision=HIGH)
```

```python
import functools

import jax
import jax.numpy as jnp
from jax import lax
from jax.experimental import pallas as pl
from jax.experimental.pallas import tpu as pltpu
from jax.sharding import Mesh
from jax.sharding import PartitionSpec as P

HIGH = lax.Precision.HIGHEST
F32 = jnp.float32
BF16 = jnp.bfloat16
PAIRS = 10
SLOT = 24
CURV = 12
LANES = 128


VMEM = pl.BlockSpec(memory_space=pltpu.VMEM)
ANY = pl.BlockSpec(memory_space=pl.ANY)
PARAMS = pltpu.CompilerParams(vmem_limit_bytes=56 * 1024 * 1024)


def call(body, out_shape, args, specs=None, scratch=(), name=None):
    many = isinstance(out_shape, (list, tuple))
    return pl.pallas_call(
        body,
        out_shape=out_shape,
        in_specs=specs or [VMEM] * len(args),
        out_specs=[VMEM] * len(out_shape) if many else VMEM,
        scratch_shapes=list(scratch),
        compiler_params=PARAMS,
        name=name,
    )(*args)


def dot(a, b, dims=((1,), (0,)), precision=HIGH):
    return lax.dot_general(a, b, (dims, ((), ())), precision=precision, preferred_element_type=F32)


def split3(value):
    hi = value.astype(BF16).astype(F32)
    rest = value - hi
    mid = rest.astype(BF16).astype(F32)
    return hi, mid, (rest - mid).astype(BF16).astype(F32)


def stack_pairs(dst, steps_ref, curv_ref):
    dst[...] = jnp.zeros(dst.shape, F32)
    dst[0:PAIRS, :] = steps_ref[...]
    dst[CURV : CURV + PAIRS, :] = curv_ref[...]


def compact_core(gram):
    gram = gram[:, :LANES]
    row = lax.broadcasted_iota(jnp.int32, gram.shape, 0)
    col = lax.broadcasted_iota(jnp.int32, gram.shape, 1)
    inv = jnp.zeros(gram.shape, F32)
    for i in reversed(range(PAIRS)):
        coef = jnp.where(row[:, 0:1] > CURV + i, gram[:, i : i + 1], 0.0)
        total = jnp.sum(coef * inv, axis=0, keepdims=True)
        unit = (col[0:1] == i).astype(F32)
        new = (unit - total) / gram[CURV + i : CURV + i + 1, i : i + 1]
        inv = jnp.where(row == CURV + i, new, inv)
    last = CURV + PAIRS - 1
    scaling = gram[last : last + 1, PAIRS - 1 : PAIRS] / gram[last : last + 1, last : last + 1]
    in_curv = (row >= CURV) & (row < CURV + PAIRS) & (col >= CURV) & (col < CURV + PAIRS)
    diag = jnp.sum(jnp.where(col == row - CURV, gram, 0.0), axis=1, keepdims=True)
    middle = jnp.where(in_curv, scaling * gram, 0.0) + jnp.where(in_curv & (row == col), diag, 0.0)
    half = dot(middle[:, :SLOT], inv)
    square = dot(inv, half, ((0,), (0,)))
    eye = (lax.broadcasted_iota(jnp.int32, (SLOT, SLOT), 0) == lax.broadcasted_iota(jnp.int32, (SLOT, SLOT), 1)).astype(F32)
    inv_t = dot(inv, eye, ((0,), (0,)))
    wide = jnp.concatenate([inv_t[:SLOT], jnp.zeros((SLOT, LANES - SLOT), F32)], axis=1)
    return scaling, square[:SLOT] - scaling * (inv + wide)


def first_body(n, grad_ref, steps_ref, curv_ref, out_ref, pairs, rows):
    tokens = grad_ref.shape[0]
    stack_pairs(pairs, steps_ref, curv_ref)
    rows[0:tokens, :] = grad_ref[...].astype(F32)
    rows[tokens : tokens + SLOT, :] = pairs[...]
    rows[tokens + SLOT :, :] = jnp.zeros((rows.shape[0] - tokens - SLOT, rows.shape[1]), F32)
    value = dot(pairs[...], rows[...], ((1,), (1,)))
    for i in range(n):
        out_ref[i] = value


def side_body(act_ref, steps_ref, curv_ref, out_ref, pairs, rows):
    tokens = act_ref.shape[0]
    stack_pairs(pairs, steps_ref, curv_ref)
    rows[0:tokens, :] = act_ref[...].astype(F32)
    rows[tokens : tokens + SLOT, :] = pairs[...]
    rows[tokens + SLOT :, :] = jnp.zeros((rows.shape[0] - tokens - SLOT, rows.shape[1]), F32)
    out_ref[...] = dot(pairs[...], rows[...], ((1,), (1,)))


def pack_body(n, parts_ref, side_ref, grad_ref, out_ref, core_ref):
    total = parts_ref[0]
    for i in range(1, parts_ref.shape[0]):
        total = total + parts_ref[i]
    tokens = grad_ref.shape[0]
    lane = lax.broadcasted_iota(jnp.int32, total.shape, 1)
    moved = pltpu.roll(total, LANES - tokens, 1)
    left = jnp.where(lane < SLOT, moved, 0.0)
    scaling, core = compact_core(left)
    core_ref[0:SLOT, :] = core
    core_ref[SLOT:, :] = jnp.broadcast_to(scaling, (core_ref.shape[0] - SLOT, LANES))
    gram = pltpu.roll(side_ref[:, LANES:], tokens, 1)
    mixed = jnp.where(lane < tokens, total, gram)
    small = jnp.concatenate([mixed, side_ref[:, 0:LANES]], axis=1)
    hi, mid, low = split3(small)
    top = jnp.concatenate([hi, low], axis=1)
    bottom = jnp.concatenate([mid, jnp.zeros(mid.shape, F32)], axis=1)
    ext = jnp.concatenate([top, bottom], axis=0).astype(BF16)
    for i in range(n):
        out_ref[i, 0:tokens, :] = grad_ref[...]
        out_ref[i, tokens:, :] = ext


def block_body(parts_ref, out_ref):
    n, rows, _ = parts_ref.shape
    tokens = rows - 2 * SLOT
    total = None
    pieces = [[], [], []]
    for i in range(n):
        out_ref[i * tokens : (i + 1) * tokens, :] = parts_ref[i, 0:tokens, :]
        ext = parts_ref[i, tokens:, :].astype(F32)
        hi, mid, low = ext[:SLOT, 0:256], ext[SLOT:, 0:256], ext[:SLOT, 256:512]
        for at, piece in enumerate((hi, mid, low)):
            pieces[at].append(piece[:, 0:tokens])
        part = hi + mid + low
        total = part if total is None else total + part
    gram = pltpu.roll(total[:, 0:LANES], LANES - tokens, 1)
    sums = split3(jnp.concatenate([total[:, LANES:], gram], axis=1))
    ext = [
        jnp.concatenate(pieces[at] + [sums[at]], axis=1) for at in range(3)
    ]
    pad = out_ref.shape[0] - n * tokens - 3 * SLOT
    ext.append(jnp.zeros((pad, out_ref.shape[1]), F32))
    out_ref[n * tokens :, :] = jnp.concatenate(ext, axis=0).astype(BF16)


def right_body(n, own, *refs):
    blocks, (out_ref, core_ref, ext, sem) = refs[: len(refs) - 4], refs[len(refs) - 4 :]
    copies = [
        pltpu.make_async_copy(b.at[pl.ds(own, 3 * SLOT), pl.ds(256, 256)], ext.at[j], sem.at[j])
        for j, b in enumerate(blocks)
    ]
    for c in copies:
        c.start()
    total = None
    for j, c in enumerate(copies):
        c.wait()
        part = ext[j].astype(F32)
        part = part[0:SLOT] + part[SLOT : 2 * SLOT] + part[2 * SLOT : 3 * SLOT]
        total = part if total is None else total + part
    for i in range(n):
        out_ref[i] = total[:, 0:LANES]
    scaling, core = compact_core(total[:, LANES:])
    core_ref[0:SLOT, :] = core
    core_ref[SLOT:, :] = jnp.broadcast_to(scaling, (core_ref.shape[0] - SLOT, LANES))


def last_body(offsets, own, act_ref, proj_ref, lcore_ref, rcore_ref, ls_ref, lc_ref, rs_ref, rc_ref, *refs):
    count = len(offsets)
    blocks = refs[:count]
    out_ref, gx, lt, aug, rhs, lhs, upair, asem, gsem = refs[count:]
    me = lax.axis_index("z")
    places = [lax.rem(me + off + count, count) for off in offsets]
    width = act_ref.shape[1]
    acopies, gcopies = [], []
    for j in range(count):
        src = act_ref.at[pl.ds(pl.multiple_of(places[j] * own, own), own), :]
        acopies.append(pltpu.make_async_copy(src, aug.at[pl.ds(j * own, own), pl.ds(0, width)], asem.at[j]))
        gcopies.append(pltpu.make_async_copy(blocks[j], gx.at[j], gsem.at[j]))
    for g in gcopies:
        g.start()
    for a in acopies:
        a.start()
    lcore = lcore_ref[0:SLOT, 0:SLOT]
    scale_l, scale_r = lcore_ref[SLOT : SLOT + 1, 0:1], rcore_ref[SLOT : SLOT + 1, 0:1]
    stack_pairs(upair, rs_ref, rc_ref)
    applied = dot(rcore_ref[0:SLOT, 0:SLOT], upair[...])
    rep = jnp.concatenate([applied] * 3 + [jnp.zeros((LANES - 3 * SLOT, width), F32)], axis=0)
    per = own // LANES
    for j in range(count):
        gcopies[j].wait()
        lt[0 : gx.shape[2], j * own : (j + 1) * own] = gx[j, 0:own, :].T
        ext = gx[j, own:, 0:own].astype(F32)
        proj = ext[0:SLOT] + ext[SLOT : 2 * SLOT] + ext[2 * SLOT : 3 * SLOT]
        cored = jnp.concatenate(split3(dot(lcore, proj)), axis=0)
        lt[gx.shape[2] :, j * own : (j + 1) * own] = cored.astype(BF16)
        au = jnp.concatenate([proj_ref[places[j] * per + k] for k in range(per)], axis=1)
        au = jnp.concatenate(list(split3(au)) + [jnp.zeros((LANES - 3 * SLOT, own), F32)], axis=0)
        aug[j * own : (j + 1) * own, width:] = au.T.astype(BF16)
    for a in acopies:
        a.wait()
    rows = gx.shape[2]
    prod = dot(lt[...], aug[...], precision=lax.Precision.DEFAULT)
    small = scale_r * prod[rows:, 0:width] + dot(prod[rows:, width:], rep)
    small = small[0:SLOT] + small[SLOT : 2 * SLOT] + small[2 * SLOT : 3 * SLOT]
    rhs[0:LANES, :] = scale_l * rep
    rhs[LANES : LANES + SLOT, :] = small
    lhs[:, 0:LANES] = prod[0:rows, width:]
    stack_l = jnp.concatenate([ls_ref[...], jnp.zeros((2, rows), F32), lc_ref[...], jnp.zeros((2, rows), F32)], axis=0)
    lhs[:, LANES : LANES + SLOT] = stack_l.T
    out_ref[...] = (scale_l * scale_r) * prod[0:rows, 0:width] + dot(lhs[...], rhs[...])


def on_device(sizes, grad_out, activations, left_steps, left_curves, right_steps, right_curves):
    ny, nc, nz, nx = sizes
    nrow = ny * nc
    row = ("y", "core")
    tokens, drow = grad_out.shape
    atok, width = activations.shape
    panel = lax.all_gather(activations, row, axis=0, tiled=True)
    sent = call(
        functools.partial(first_body, nrow),
        jax.ShapeDtypeStruct((nrow, SLOT, LANES), F32),
        (grad_out, left_steps, left_curves),
        scratch=(pltpu.VMEM((SLOT, drow), F32), pltpu.VMEM((LANES, drow), F32)),
        name="first",
    )
    parts = lax.all_to_all(sent, row, 0, 0, tiled=True)
    side = call(
        side_body,
        jax.ShapeDtypeStruct((SLOT, 2 * LANES), F32),
        (activations, right_steps, right_curves),
        scratch=(pltpu.VMEM((SLOT, width), F32), pltpu.VMEM((2 * LANES, width), F32)),
        name="side",
    )
    packed, lcore = call(
        functools.partial(pack_body, nx),
        (
            jax.ShapeDtypeStruct((nx, tokens + 2 * SLOT, drow), BF16),
            jax.ShapeDtypeStruct((SLOT + 8, LANES), F32),
        ),
        (parts, side, grad_out),
        name="pack",
    )
    alongx = lax.all_to_all(packed, "x", 0, 0, tiled=True)
    own = nx * tokens
    block = call(
        block_body,
        jax.ShapeDtypeStruct((own + 80, drow), BF16),
        (alongx,),
        name="block",
    )

    def shift(value, by):
        return lax.ppermute(value, "z", [(i, (i + by) % nz) for i in range(nz)])

    blocks, offsets = [block], [0]
    up = down = block
    for k in range(1, nz // 2):
        up, down = shift(up, 1), shift(down, -1)
        blocks += [up, down]
        offsets += [-k, k]
    blocks.append(shift(up, 1))
    offsets.append(-(nz // 2))
    gath, rcore = call(
        functools.partial(right_body, nrow, own),
        (
            jax.ShapeDtypeStruct((nrow, SLOT, LANES), F32),
            jax.ShapeDtypeStruct((SLOT + 8, LANES), F32),
        ),
        tuple(blocks),
        specs=[ANY] * nz,
        scratch=(pltpu.VMEM((nz, 3 * SLOT, 256), BF16), pltpu.SemaphoreType.DMA((nz,))),
        name="right",
    )
    proj = lax.all_to_all(gath, row, 0, 0, tiled=True)
    total = own * nz
    return call(
        functools.partial(last_body, tuple(offsets), own),
        jax.ShapeDtypeStruct((drow, width), F32),
        (panel, proj, lcore, rcore, left_steps, left_curves, right_steps, right_curves, *blocks),
        specs=[ANY] + [VMEM] * 7 + [ANY] * nz,
        scratch=(
            pltpu.VMEM((nz, own + 80, drow), BF16),
            pltpu.VMEM((drow + 3 * SLOT, total), BF16),
            pltpu.VMEM((total, width + LANES), BF16),
            pltpu.VMEM((LANES + SLOT, width), F32),
            pltpu.VMEM((drow, LANES + SLOT), F32),
            pltpu.VMEM((SLOT, width), F32),
            pltpu.SemaphoreType.DMA((nz,)),
            pltpu.SemaphoreType.DMA((nz,)),
        ),
        name="last",
    )


def solution(mesh):
    devices = mesh.devices
    sizes = (devices.shape[0] // 2, 2, 8, devices.shape[1] // 8)
    mesh = Mesh(devices.reshape(sizes), ("y", "core", "z", "x"))
    row, col = ("y", "core"), ("z", "x")
    in_specs = (P(col, row), P(row, col), P(None, row), P(None, row), P(None, col), P(None, col))
    return jax.shard_map(
        functools.partial(on_device, sizes),
        mesh=mesh,
        in_specs=in_specs,
        out_specs=P(row, col),
        check_vma=False,
    )
```
